512 devices in a mesh: section: 8 (over y, core), mp: 64 (over z, x).
Axes of the slice: x: 4, y: 4, z: 16, core: 2. Of those that a mesh axis runs over, the one named last changes fastest.
Arguments:
- features: bfloat16 [4, 32, 8192], P(None, None, 'mp'), may hold values from -6 to 6
- labels: int32 [4, 32], replicated, may hold values 0 or 1
- weights: bfloat16 [8, 8192, 8192], P('section', None, 'mp'), may hold values from -1.78986404 to 1.78986404
- vectors: float32 [8, 8192], P('section', 'mp'), may hold values from -6 to 6
- head_weight: float32 [8192], P('mp'), may hold values from -0.0625 to 0.0625
Outputs:
- weight_grad: bfloat16 [8, 8192, 8192], P('section', None, 'mp')
- new_vectors: float32 [8, 8192], P('section', 'mp')
- rank_coef: float32 [8], P('section')
The draws below stay inside these ranges and needn't reach their ends.
All inputs are finite; a program needn't handle non-finite values.
Results may differ from the reference program's by a relative error of at most 0.015.
Values may be sent and summed in bfloat16 or wider, within the bound.
A program may use at most 64 MiB of HBM per device.

```python
import math
import jax
import jax.numpy as jnp
from jax import lax

D = 8192
MICRO = 4
BATCH = 32
LAYERS = 8


def draw_weights(key, part):
    key_base = jax.random.fold_in(key, 11)
    key_list = jax.random.split(key_base, 3)
    base_draw = jnp.clip(jax.random.normal(key_list[0], (LAYERS, D, D), jnp.float32), -6.0, 6.0)
    low_scale = 0.5
    high_scale = 2.0
    row_scale = jnp.exp(jax.random.uniform(key_list[1], (LAYERS, D, 1), jnp.float32, math.log(low_scale), math.log(high_scale)))
    col_scale = jnp.exp(jax.random.uniform(key_list[2], (LAYERS, 1, D), jnp.float32, math.log(low_scale), math.log(high_scale)))
    col_ramp = jnp.exp(math.log(3.0) * jnp.arange(D, dtype=jnp.float32) / D)
    scaled = base_draw * row_scale * col_scale * col_ramp[None, None, :] / math.sqrt(D)
    return scaled.astype(jnp.bfloat16)


def with_ends(values, key, smallest, largest):
    longest = values.shape.index(max(values.shape))
    spots = []
    for shift in (0, 1):
        where = [jax.random.randint(jax.random.fold_in(key, axis), (), 0, length) for axis, length in enumerate(values.shape)]
        where[longest] = (where[longest] + shift) % values.shape[longest]
        spots.append(tuple(where))
    return values.at[spots[0]].set(smallest).at[spots[1]].set(largest)


def levels(stream_key, dims, shards, smallest, top_value):
    def one(position, shards_of):
        steps = jax.random.uniform(jax.random.fold_in(jax.random.fold_in(stream_key, 6), position), (shards_of,), jnp.float32, smallest / len(shards), top_value / len(shards))
        return jnp.repeat(jnp.exp(steps), dims[position] // shards_of).reshape((-1,) + (1,) * (len(dims) - position - 1))

    factor_of = one(*shards[0])
    for cut in shards[1:]:
        factor_of = factor_of * one(*cut)
    return factor_of


def normal_values(own_key, dims, spread, reach, shards=(), kind=jnp.bfloat16):
    array = spread * jax.random.normal(own_key, dims, jnp.float32)
    if shards:
        array = array * levels(own_key, dims, shards, -0.22, 0.18)
    return jnp.clip(array, -reach, reach).astype(kind)


def setup_inputs(seed: int = 0) -> dict:
    seeds = jax.random.split(jax.random.key(seed), 6)
    features = normal_values(seeds[0], (MICRO, BATCH, D), 1.0, 6.0, ((2, 64),))
    labels = with_ends((jax.random.randint(seeds[1], (MICRO, BATCH), 0, 2) < 1).astype(jnp.int32), jax.random.fold_in(seeds[1], 1), 0, 1)
    weights = draw_weights(jax.random.fold_in(seeds[5], 71), 0)
    vectors = normal_values(seeds[3], (LAYERS, D), 1.0, 6.0, ((0, 8), (1, 64)), jnp.float32)
    head_weight = normal_values(seeds[4], (D,), D ** -0.5, 0.0625, ((0, 64),), jnp.float32)
    return dict(features=features, labels=labels, weights=weights, vectors=vectors, head_weight=head_weight)


loss_scale = 32.0
tiny_eps = 1e-06

def silu_slope(pre_act):
    gate_val = jax.nn.sigmoid(pre_act)
    return gate_val * (1.0 + pre_act * (1.0 - gate_val))

def reference(features, labels, weights, vectors, head_weight):
    micro_count, batch_rows, full_width = features.shape
    layer_count = weights.shape[0]
    hidden = features.reshape(micro_count * batch_rows, full_width)
    sign_all = (2 * labels - 1).astype(jnp.float32).reshape(-1)
    sigmas = []
    new_list = []
    inputs = []
    pre_acts = []
    for layer_index in range(layer_count):
        weight = weights[layer_index]
        vector_bf = vectors[layer_index].astype(jnp.bfloat16)
        left_sum = jnp.dot(weight, vector_bf, preferred_element_type=jnp.float32)
        vector_v = (left_sum * lax.rsqrt(jnp.sum(left_sum * left_sum) + tiny_eps)).astype(jnp.bfloat16)
        right_part = jnp.dot(vector_v, weight, preferred_element_type=jnp.float32)
        spectral = jnp.sqrt(jnp.sum(right_part * right_part) + tiny_eps)
        sigmas.append(spectral)
        new_list.append(right_part / spectral)
        pre_act = jnp.dot(hidden, weight, preferred_element_type=jnp.float32) / spectral
        inputs.append(hidden)
        pre_acts.append(pre_act)
        hidden = (hidden.astype(jnp.float32) + jax.nn.silu(pre_act)).astype(jnp.bfloat16)
    logit_row = lax.optimization_barrier(jnp.sum(hidden.astype(jnp.float32) * head_weight[None, :], axis=1))
    top_scale = -loss_scale * sign_all * jax.nn.sigmoid(-sign_all * logit_row)
    grad_hidden = (top_scale[:, None] * head_weight[None, :]).astype(jnp.bfloat16)
    grad_list = [None] * layer_count
    coef_list = [None] * layer_count
    for layer_index in reversed(range(layer_count)):
        weight = weights[layer_index]
        spectral = sigmas[layer_index]
        grad_pre = (grad_hidden.astype(jnp.float32) * silu_slope(pre_acts[layer_index])).astype(jnp.bfloat16)
        outer_sum = jnp.dot(inputs[layer_index].T, grad_pre, preferred_element_type=jnp.float32)
        grad_list[layer_index] = (outer_sum / spectral).astype(jnp.bfloat16)
        coef_list[layer_index] = jnp.sum(outer_sum * weight.astype(jnp.float32)) / (spectral * spectral)
        if layer_index > 0:
            back_sum = jnp.dot(grad_pre, weight.T, preferred_element_type=jnp.float32)
            grad_hidden = (grad_hidden.astype(jnp.float32) + back_sum / spectral).astype(jnp.bfloat16)
    return (jnp.stack(grad_list), jnp.stack(new_list), jnp.stack(coef_list))
```

```python
import functools

import jax
import jax.numpy as jnp
from jax import lax
from jax.experimental import pallas as pl
from jax.experimental.pallas import tpu as pltpu
from jax.sharding import Mesh
from jax.sharding import PartitionSpec as P

MP = ("mp_0", "mp_1")
loss_scale = 32.0
tiny_eps = 1e-06
LANES = 128


def silu_slope(pre_act):
    gate_val = jax.nn.sigmoid(pre_act)
    return gate_val * (1.0 + pre_act * (1.0 - gate_val))


def far_first(count):
    return sorted(range(count), key=lambda d: -min(d, count - d))


def remote(src, dst, send, recv, device):
    return pltpu.make_async_remote_copy(
        src_ref=src,
        dst_ref=dst,
        send_sem=send,
        recv_sem=recv,
        device_id=device,
        device_id_type=pl.DeviceIdType.MESH,
    )


def await_bytes(ref, sem):
    pltpu.make_async_copy(ref, ref, sem).wait()


def step_kernel(
    dims,
    feat,
    labels,
    w,
    u,
    head,
    wg_out,
    nu_out,
    coef_out,
    hid,
    hout,
    pre,
    gpre,
    ghid,
    part,
    part_in,
    colsum,
    col_in,
    gh_in,
    left_x,
    left_xin,
    left_z,
    left_zin,
    left_all,
    norm_z,
    norm_x,
    logit_z,
    logit_x,
    coef_z,
    coef_x,
    inv_sig,
    small_send,
    small_recv,
    fz_send,
    fz_recv,
    fx_send,
    fx_recv,
    bx_send,
    bx_recv,
    bz_send,
    bz_recv,
    bg_send,
    bg_recv,
    lz_send,
    lz_recv,
    lx_send,
    lx_recv,
):
    S, Z, X, n, R = dims
    s = lax.axis_index("section")
    z = lax.axis_index("mp_0")
    x = lax.axis_index("mp_1")
    nxt = lax.rem(s + 1, S)
    prv = lax.rem(s + S - 1, S)
    z_far = far_first(Z)

    def zat(d):
        return lax.rem(z + d, Z)

    def xat(d):
        return lax.rem(x + d, X)

    barrier = pltpu.get_barrier_semaphore()

    def greet(device):
        pl.semaphore_signal(
            barrier, inc=1, device_id=device, device_id_type=pl.DeviceIdType.MESH
        )

    for d in z_far:
        greet((nxt, zat(d), x))
        greet((prv, zat(d), x))
        if d:
            greet((s, zat(d), x))
    for d in range(1, X):
        greet((s, z, xat(d)))

    u_rows = jnp.broadcast_to(u[...], (16, LANES)).astype(jnp.bfloat16)

    def left_block(zi, carry):
        for xi in range(X):
            block = lax.dot_general(
                u_rows, w[zi * X + xi], (((1,), (1,)), ((), ())),
                preferred_element_type=jnp.float32,
            )
            left_x[xi, zi] = block[0:1]
        return carry

    lax.fori_loop(0, Z, left_block, 0)
    pl.semaphore_wait(barrier, 3 * Z - 1 + X - 1)

    @pl.when(s == S - 1)
    def _():
        def send_features(m, carry):
            for d in z_far:
                remote(
                    feat.at[m], hid.at[m, x, z], fz_send.at[m], fz_recv.at[m], (nxt, zat(d), x)
                ).start()
            return carry

        lax.fori_loop(0, n, send_features, 0)

    def spread_z(src, dst, k):
        for d in z_far:
            if d:
                remote(src(d), dst, small_send.at[k], small_recv.at[k], (s, zat(d), x)).start()

    def spread_x(src, dst, k):
        for d in range(1, X):
            remote(src(d), dst, small_send.at[k], small_recv.at[k], (s, z, xat(d))).start()

    spread_x(lambda d: left_x.at[xat(d)], left_xin.at[x], 0)
    await_bytes(left_xin.at[pl.ds(0, X - 1)], small_recv.at[0])
    column = left_x[x]
    for d in range(1, X):
        column = column + left_xin[xat(d)]
    left_z[...] = column
    spread_z(lambda d: left_z.at[zat(d)], left_zin.at[z], 1)
    await_bytes(left_zin.at[pl.ds(0, Z - 1)], small_recv.at[1])
    left_zin[z] = left_z[z]
    left_all[x, z] = jnp.sum(left_zin[...], axis=0)
    spread_z(lambda d: left_all.at[x, z], left_all.at[x, z], 2)

    def forward_columns(m):
        await_bytes(hid.at[m, x], fz_recv.at[m])
        for d in range(1, X):
            remote(
                hid.at[m, x], hid.at[m, x], fx_send.at[m], fx_recv.at[m, x], (s, z, xat(d))
            ).start()

    @pl.when(s == 0)
    def _():
        def pass_on(m, carry):
            forward_columns(m)
            return carry

        lax.fori_loop(0, n, pass_on, 0)

    await_bytes(left_all.at[0, pl.ds(0, Z - 1)], small_recv.at[2])
    spread_x(lambda d: left_all.at[x], left_all.at[x], 3)
    await_bytes(left_all.at[pl.ds(0, X - 1)], small_recv.at[3])

    left = left_all[...]
    total = jnp.sum(jnp.sum(left * left, axis=(0, 1)), axis=-1, keepdims=True)
    scale_v = lax.rsqrt(total + tiny_eps)

    def pair(ref_rows):
        return jnp.concatenate(ref_rows, axis=1)

    def w_pair(xi, zi):
        return jnp.concatenate([w[zi * X + xi], w[(zi + 1) * X + xi]], axis=0)

    def right_block(zp, acc):
        zi = zp * 2
        for xi in range(X):
            rows = [
                jnp.broadcast_to(left_all[xi, zi + k] * scale_v, (16, LANES)).astype(jnp.bfloat16)
                for k in range(2)
            ]
            acc = acc + jnp.dot(pair(rows), w_pair(xi, zi), preferred_element_type=jnp.float32)
        return acc

    right = lax.fori_loop(0, Z // 2, right_block, jnp.zeros((16, LANES), jnp.float32))[0:1]

    def all_sum(value, zbuf, xbuf, kz, kx):
        zbuf[z] = value
        spread_z(lambda d: zbuf.at[z], zbuf.at[z], kz)
        await_bytes(zbuf.at[pl.ds(0, Z - 1)], small_recv.at[kz])
        xbuf[x] = jnp.sum(zbuf[...], axis=0)
        spread_x(lambda d: xbuf.at[x], xbuf.at[x], kx)
        await_bytes(xbuf.at[pl.ds(0, X - 1)], small_recv.at[kx])
        return jnp.sum(jnp.sum(xbuf[...], axis=0), axis=-1, keepdims=True)

    norm_total = all_sum(right * right, norm_z, norm_x, 4, 5)
    inv = 1.0 / jnp.sqrt(norm_total + tiny_eps)
    inv_sig[...] = jnp.broadcast_to(inv, (1, LANES))
    nu_out[...] = right * inv

    def forward_micro(m, carry):
        @pl.when(s > 0)
        def _():
            forward_columns(m)

        acc = jnp.zeros((R, LANES), jnp.float32)
        for d in range(X):
            xi = xat(d)
            if d:
                await_bytes(hid.at[m, xi], fx_recv.at[m, xi])
            for zi in range(0, Z, 2):
                acc = acc + jnp.dot(
                    pair([hid[m, xi, zi], hid[m, xi, zi + 1]]), w_pair(xi, zi),
                    preferred_element_type=jnp.float32,
                )
        pre_act = acc * inv_sig[...]
        pre[m] = pre_act
        out = (hid[m, x, z].astype(jnp.float32) + pre_act * jax.nn.sigmoid(pre_act)).astype(
            jnp.bfloat16
        )
        hout[m] = out

        @pl.when(s < S - 1)
        def _():
            for d in z_far:
                remote(
                    hout.at[m], hid.at[m, x, z], fz_send.at[m], fz_recv.at[m], (nxt, zat(d), x)
                ).start()

        @pl.when(s == S - 1)
        def _():
            terms = jnp.sum(out.astype(jnp.float32) * head[...], axis=1, keepdims=True)
            lane = lax.broadcasted_iota(jnp.int32, (R, LANES), 1)
            row = lax.broadcasted_iota(jnp.int32, (R, LANES), 0)
            spread = jnp.where(lane == row, jnp.broadcast_to(terms, (R, LANES)), 0.0)
            logit_z[m, z] = jnp.sum(spread, axis=0, keepdims=True)
            for d in z_far:
                if d:
                    remote(
                        logit_z.at[m, z], logit_z.at[m, z], lz_send.at[m], lz_recv.at[m],
                        (s, zat(d), x),
                    ).start()

        return carry

    lax.fori_loop(0, n, forward_micro, 0)

    def backward_micro(m, carry):
        @pl.when(s == S - 1)
        def _():
            await_bytes(logit_z.at[m, pl.ds(0, Z - 1)], lz_recv.at[m])
            logit_x[m, x] = jnp.sum(logit_z[m], axis=0)
            for d in range(1, X):
                remote(
                    logit_x.at[m, x], logit_x.at[m, x], lx_send.at[m], lx_recv.at[m],
                    (s, z, xat(d)),
                ).start()
            await_bytes(logit_x.at[m, pl.ds(0, X - 1)], lx_recv.at[m])
            logit_row = jnp.sum(logit_x[m], axis=0)
            lane = lax.broadcasted_iota(jnp.int32, (R, LANES), 1)
            row = lax.broadcasted_iota(jnp.int32, (R, LANES), 0)
            sign_row = (2 * labels[m] - 1).astype(jnp.float32)
            top_row = -loss_scale * sign_row * jax.nn.sigmoid(-sign_row * logit_row)
            top = jnp.sum(
                jnp.where(lane == row, jnp.broadcast_to(top_row, (R, LANES)), 0.0),
                axis=1, keepdims=True,
            )
            ghid[m] = (top * head[...]).astype(jnp.bfloat16)

        @pl.when(s < S - 1)
        def _():
            await_bytes(col_in.at[m], bz_recv.at[m])
            await_bytes(gh_in.at[m], bg_recv.at[m])
            back = jnp.sum(col_in[m].astype(jnp.float32), axis=0)
            ghid[m] = (gh_in[m].astype(jnp.float32) + back).astype(jnp.bfloat16)

        grad = (ghid[m].astype(jnp.float32) * silu_slope(pre[m])).astype(jnp.bfloat16)
        gpre[m] = grad

        @pl.when(s > 0)
        def _():
            remote(
                ghid.at[m], gh_in.at[m], bg_send.at[m], bg_recv.at[m], (prv, z, x)
            ).start()
            for d in [*range(1, X), 0]:
                xi = xat(d)
                for zi in range(Z):
                    part[m, xi, zi] = lax.dot_general(
                        grad, w[zi * X + xi], (((1,), (1,)), ((), ())),
                        preferred_element_type=jnp.float32,
                    ).astype(jnp.bfloat16)
                if d:
                    remote(
                        part.at[m, xi], part_in.at[m, x], bx_send.at[m], bx_recv.at[m],
                        (s, z, xi),
                    ).start()
            await_bytes(part_in.at[m, pl.ds(0, X - 1)], bx_recv.at[m])
            for d in z_far:
                zi = zat(d)
                column_sum = part[m, x, zi].astype(jnp.float32)
                for e in range(1, X):
                    column_sum = column_sum + part_in[m, xat(e), zi].astype(jnp.float32)
                colsum[m, zi] = (column_sum * inv_sig[...]).astype(jnp.bfloat16)
            for d in z_far:
                zi = zat(d)
                remote(
                    colsum.at[m, zi], col_in.at[m, z], bz_send.at[m], bz_recv.at[m], (prv, zi, x)
                ).start()

        return carry

    lax.fori_loop(0, n, backward_micro, 0)

    inner = jnp.sum(gpre[...].astype(jnp.float32) * pre[...], axis=0)
    coef_z[z] = jnp.sum(inner, axis=0, keepdims=True)
    spread_z(lambda d: coef_z.at[z], coef_z.at[z], 6)

    grads = gpre[...].reshape(n * R, LANES)

    def weight_block(zi, carry):
        for xi in range(X):
            rows = hid[:, xi, zi].reshape(n * R, LANES)
            block = lax.dot_general(
                rows, grads, (((0,), (0,)), ((), ())), preferred_element_type=jnp.float32
            )
            wg_out[zi * X + xi] = (block * inv_sig[...]).astype(jnp.bfloat16)
        return carry

    lax.fori_loop(0, Z, weight_block, 0)

    await_bytes(coef_z.at[pl.ds(0, Z - 1)], small_recv.at[6])
    coef_x[x] = jnp.sum(coef_z[...], axis=0)
    spread_x(lambda d: coef_x.at[x], coef_x.at[x], 7)
    await_bytes(coef_x.at[pl.ds(0, X - 1)], small_recv.at[7])
    inner_total = jnp.sum(jnp.sum(coef_x[...], axis=0), axis=-1, keepdims=True)
    coef_out[...] = inner_total * inv_sig[...]

    await_bytes(left_xin.at[pl.ds(0, X - 1)], small_send.at[0])
    await_bytes(left_zin.at[pl.ds(0, Z - 1)], small_send.at[1])
    await_bytes(left_zin.at[pl.ds(0, Z - 1)], small_send.at[2])
    await_bytes(left_xin.at[pl.ds(0, X - 1)], small_send.at[3])
    for k, buf in ((4, norm_z), (6, coef_z)):
        await_bytes(buf.at[pl.ds(0, Z - 1)], small_send.at[k])
    for k, buf in ((5, norm_x), (7, coef_x)):
        await_bytes(buf.at[pl.ds(0, X - 1)], small_send.at[k])

    def drain(m, carry):
        await_bytes(hid.at[m, 0], fz_send.at[m])
        await_bytes(hid.at[m, pl.ds(0, X - 1)], fx_send.at[m])

        @pl.when(s > 0)
        def _():
            await_bytes(ghid.at[m], bg_send.at[m])
            await_bytes(part_in.at[m, pl.ds(0, X - 1)], bx_send.at[m])
            await_bytes(colsum.at[m], bz_send.at[m])

        @pl.when(s == S - 1)
        def _():
            await_bytes(logit_z.at[m, pl.ds(0, Z - 1)], lz_send.at[m])
            await_bytes(logit_x.at[m, pl.ds(0, X - 1)], lx_send.at[m])

        return carry

    lax.fori_loop(0, n, drain, 0)


def on_device(features, labels, weights, vectors, head_weight):
    S, Z, X = lax.axis_size("section"), lax.axis_size("mp_0"), lax.axis_size("mp_1")
    n, R, _ = features.shape
    blocks = Z * X
    bf, f32 = jnp.bfloat16, jnp.float32
    label_rows = jnp.pad(labels[:, None, :], ((0, 0), (0, 0), (0, LANES - R)))
    vmem = pl.BlockSpec(memory_space=pltpu.VMEM)
    dma = pltpu.SemaphoreType.DMA
    wg, nu, coef = pl.pallas_call(
        functools.partial(step_kernel, (S, Z, X, n, R)),
        out_shape=(
            jax.ShapeDtypeStruct((blocks, LANES, LANES), bf),
            jax.ShapeDtypeStruct((1, LANES), f32),
            jax.ShapeDtypeStruct((1, LANES), f32),
        ),
        in_specs=[vmem] * 5,
        out_specs=(vmem, vmem, vmem),
        scratch_shapes=[
            pltpu.VMEM((n, X, Z, R, LANES), bf),
            pltpu.VMEM((n, R, LANES), bf),
            pltpu.VMEM((n, R, LANES), f32),
            pltpu.VMEM((n, R, LANES), bf),
            pltpu.VMEM((n, R, LANES), bf),
            pltpu.VMEM((n, X, Z, R, LANES), bf),
            pltpu.VMEM((n, X, Z, R, LANES), bf),
            pltpu.VMEM((n, Z, R, LANES), bf),
            pltpu.VMEM((n, Z, R, LANES), bf),
            pltpu.VMEM((n, R, LANES), bf),
            pltpu.VMEM((X, Z, 1, LANES), f32),
            pltpu.VMEM((X, Z, 1, LANES), f32),
            pltpu.VMEM((Z, 1, LANES), f32),
            pltpu.VMEM((Z, 1, LANES), f32),
            pltpu.VMEM((X, Z, 1, LANES), f32),
            pltpu.VMEM((Z, 1, LANES), f32),
            pltpu.VMEM((X, 1, LANES), f32),
            pltpu.VMEM((n, Z, 1, LANES), f32),
            pltpu.VMEM((n, X, 1, LANES), f32),
            pltpu.VMEM((Z, 1, LANES), f32),
            pltpu.VMEM((X, 1, LANES), f32),
            pltpu.VMEM((1, LANES), f32),
            dma((8,)),
            dma((8,)),
            dma((n,)),
            dma((n,)),
            dma((n,)),
            dma((n, X)),
            dma((n,)),
            dma((n,)),
            dma((n,)),
            dma((n,)),
            dma((n,)),
            dma((n,)),
            dma((n,)),
            dma((n,)),
            dma((n,)),
            dma((n,)),
        ],
        compiler_params=pltpu.CompilerParams(collective_id=0, has_side_effects=True),
    )(
        features,
        label_rows,
        weights.reshape(blocks, LANES, LANES),
        vectors,
        head_weight[None],
    )
    return wg.reshape(1, blocks * LANES, LANES), nu, coef[0, :1]


def solution(mesh):
    columns = [4 if mesh.shape["mp"] == 64 else 2]
    x_size = columns[0]
    sections = mesh.shape["section"]
    torus = Mesh(
        mesh.devices.reshape(sections, mesh.shape["mp"] // x_size, x_size),
        ("section", "mp_0", "mp_1"),
    )
    placed = (P(None, None, MP), P(), P("section", None, MP), P("section", MP), P(MP))
    return jax.shard_map(
        on_device,
        mesh=torus,
        in_specs=placed,
        out_specs=(P("section", None, MP), P("section", MP), P("section")),
        check_vma=False,
    )
```

```python
import functools

import jax
import jax.numpy as jnp
from jax import lax
from jax.experimental import pallas as pl
from jax.experimental.pallas import tpu as pltpu
from jax.sharding import Mesh
from jax.sharding import PartitionSpec as P

MP = ("mp_0", "mp_1")
loss_scale = 32.0
tiny_eps = 1e-06
LANES = 128


def silu_slope(pre_act):
    gate_val = jax.nn.sigmoid(pre_act)
    return gate_val * (1.0 + pre_act * (1.0 - gate_val))


def near_first(count):
    return sorted(range(count), key=lambda d: min(d, count - d))


def remote(src, dst, send, recv, device):
    return pltpu.make_async_remote_copy(
        src_ref=src,
        dst_ref=dst,
        send_sem=send,
        recv_sem=recv,
        device_id=device,
        device_id_type=pl.DeviceIdType.MESH,
    )


def await_bytes(ref, sem):
    pltpu.make_async_copy(ref, ref, sem).wait()


def step_kernel(
    dims,
    feat,
    labels,
    w_hbm,
    u,
    head,
    wg_out,
    nu_out,
    coef_out,
    w,
    w_sem,
    hid,
    hout,
    pre,
    gpre,
    ghid,
    part,
    part_in,
    colsum,
    col_in,
    gh_in,
    left_x,
    left_xin,
    left_zin,
    left_all,
    norm_z,
    norm_x,
    logit_z,
    logit_x,
    coef_z,
    coef_x,
    inv_sig,
    small_send,
    small_recv,
    fz_send,
    fz_recv,
    fx_send,
    fx_recv,
    bx_send,
    bx_recv,
    bz_send,
    bz_recv,
    bg_send,
    bg_recv,
    lz_send,
    lz_recv,
    lx_send,
    lx_recv,
):
    S, Z, X, n, R = dims
    near = near_first(Z)
    z_far = near[::-1]
    slot_of = {d: k for k, d in enumerate(near)}
    groups = [(0, Z // 2), (Z // 2, Z // 4), (Z // 2 + Z // 4, Z // 4)]
    group_of = [0] * (Z // 2) + [1] * (Z // 4) + [2] * (Z // 4)
    s = lax.axis_index("section")
    z = lax.axis_index("mp_0")
    x = lax.axis_index("mp_1")
    nxt = lax.rem(s + 1, S)
    prv = lax.rem(s + S - 1, S)
    x_far = near_first(X)[:0:-1]

    def zat(d):
        return lax.rem(z + d, Z)

    def xat(d):
        return lax.rem(x + d, X)

    barrier = pltpu.get_barrier_semaphore()

    def greet(device):
        pl.semaphore_signal(
            barrier, inc=1, device_id=device, device_id_type=pl.DeviceIdType.MESH
        )

    for d in z_far:
        greet((nxt, zat(d), x))
        greet((prv, zat(d), x))
        if d:
            greet((s, zat(d), x))
    for d in range(1, X):
        greet((s, z, xat(d)))

    load_w = pltpu.make_async_copy(w_hbm, w, w_sem)
    load_w.start()
    z_slot = [zat(d) for d in near]
    u_rows = jnp.broadcast_to(u[...], (16, LANES)).astype(jnp.bfloat16)

    def left_block(zi, carry):
        for xi in range(X):
            block = lax.dot_general(
                u_rows, w[zi * X + xi], (((1,), (1,)), ((), ())),
                preferred_element_type=jnp.float32,
            )
            left_x[xi, zi] = block[0:1]
        return carry

    load_w.wait()
    lax.fori_loop(0, Z, left_block, 0)
    pl.semaphore_wait(barrier, 3 * Z - 1 + X - 1)

    @pl.when(s == S - 1)
    def _():
        def send_features(m, carry):
            for d in z_far:
                k = slot_of[(Z - d) % Z]
                remote(
                    feat.at[m], hid.at[m, x, k], fz_send.at[m], fz_recv.at[m, group_of[k]],
                    (nxt, zat(d), x),
                ).start()
            return carry

        lax.fori_loop(0, n, send_features, 0)

    def spread_z(src, dst, k):
        for d in z_far:
            if d:
                remote(src(d), dst, small_send.at[k], small_recv.at[k], (s, zat(d), x)).start()

    def spread_x(src, dst, k):
        for d in range(1, X):
            remote(src(d), dst, small_send.at[k], small_recv.at[k], (s, z, xat(d))).start()

    spread_x(lambda d: left_x.at[xat(d)], left_xin.at[x], 0)
    await_bytes(left_xin.at[pl.ds(0, X - 1)], small_recv.at[0])
    column = left_x[x]
    for d in range(1, X):
        column = column + left_xin[xat(d)]
    left_zin[z] = column
    spread_z(lambda d: left_zin.at[z], left_zin.at[z], 1)

    def forward_columns(m):
        for g, (first, size) in enumerate(groups):
            slots = pl.ds(first, size)
            await_bytes(hid.at[m, x, slots], fz_recv.at[m, g])
            for d in x_far:
                remote(
                    hid.at[m, x, slots], hid.at[m, x, slots], fx_send.at[m], fx_recv.at[m, g],
                    (s, z, xat(d)),
                ).start()

    await_bytes(left_zin.at[pl.ds(0, Z - 1)], small_recv.at[1])
    left_all[x] = jnp.sum(left_zin[...], axis=0)
    spread_x(lambda d: left_all.at[x], left_all.at[x], 3)
    await_bytes(left_all.at[pl.ds(0, X - 1)], small_recv.at[3])

    left = left_all[...]
    total = jnp.sum(jnp.sum(left * left, axis=(0, 1)), axis=-1, keepdims=True)
    scale_v = lax.rsqrt(total + tiny_eps)

    def pair(ref_rows):
        return jnp.concatenate(ref_rows, axis=1)

    def w_pair(xi, zi):
        return jnp.concatenate([w[zi * X + xi], w[(zi + 1) * X + xi]], axis=0)

    def right_block(zp, acc):
        zi = zp * 2
        for xi in range(X):
            rows = [
                jnp.broadcast_to(left_all[xi, zi + k] * scale_v, (16, LANES)).astype(jnp.bfloat16)
                for k in range(2)
            ]
            acc = acc + jnp.dot(pair(rows), w_pair(xi, zi), preferred_element_type=jnp.float32)
        return acc

    right = lax.fori_loop(0, Z // 2, right_block, jnp.zeros((16, LANES), jnp.float32))[0:1]

    norm_z[z] = right * right
    spread_z(lambda d: norm_z.at[z], norm_z.at[z], 4)

    @pl.when(s == 0)
    def _():
        def pass_on(m, carry):
            forward_columns(m)
            return carry

        lax.fori_loop(0, n, pass_on, 0)

    await_bytes(norm_z.at[pl.ds(0, Z - 1)], small_recv.at[4])
    norm_x[x] = jnp.sum(norm_z[...], axis=0)
    spread_x(lambda d: norm_x.at[x], norm_x.at[x], 5)
    await_bytes(norm_x.at[pl.ds(0, X - 1)], small_recv.at[5])
    norm_total = jnp.sum(jnp.sum(norm_x[...], axis=0), axis=-1, keepdims=True)
    inv = 1.0 / jnp.sqrt(norm_total + tiny_eps)
    inv_sig[...] = jnp.broadcast_to(inv, (1, LANES))
    nu_out[...] = right * inv

    def forward_micro(m, carry):
        @pl.when(s > 0)
        def _():
            forward_columns(m)

        def partial_dots(acc, d, first, size):
            xi = xat(d)
            for k in range(first, first + size, 2):
                rows = jnp.concatenate([hid[m, xi, k], hid[m, xi, k + 1]], axis=1)
                cols = jnp.concatenate(
                    [w[z_slot[k] * X + xi], w[z_slot[k + 1] * X + xi]], axis=0
                )
                acc = acc + jnp.dot(rows, cols, preferred_element_type=jnp.float32)
            return acc

        acc = partial_dots(jnp.zeros((R, LANES), jnp.float32), 0, 0, Z)
        for g, (first, size) in enumerate(groups):
            await_bytes(hid.at[m, pl.ds(0, X - 1), pl.ds(first, size)], fx_recv.at[m, g])
            for d in range(1, X):
                acc = partial_dots(acc, d, first, size)
        pre_act = acc * inv_sig[...]
        pre[m] = pre_act
        out = (hid[m, x, 0].astype(jnp.float32) + pre_act * jax.nn.sigmoid(pre_act)).astype(
            jnp.bfloat16
        )
        hout[m] = out

        @pl.when(s < S - 1)
        def _():
            for d in z_far:
                k = slot_of[(Z - d) % Z]
                remote(
                    hout.at[m], hid.at[m, x, k], fz_send.at[m], fz_recv.at[m, group_of[k]],
                    (nxt, zat(d), x),
                ).start()

        @pl.when(s == S - 1)
        def _():
            terms = jnp.sum(out.astype(jnp.float32) * head[...], axis=1, keepdims=True)
            lane = lax.broadcasted_iota(jnp.int32, (R, LANES), 1)
            row = lax.broadcasted_iota(jnp.int32, (R, LANES), 0)
            spread = jnp.where(lane == row, jnp.broadcast_to(terms, (R, LANES)), 0.0)
            logit_z[m, z] = jnp.sum(spread, axis=0, keepdims=True)
            for d in z_far:
                if d:
                    remote(
                        logit_z.at[m, z], logit_z.at[m, z], lz_send.at[m], lz_recv.at[m],
                        (s, zat(d), x),
                    ).start()

        return carry

    def backward_micro(m, carry):
        @pl.when(s == S - 1)
        def _():
            await_bytes(logit_z.at[m, pl.ds(0, Z - 1)], lz_recv.at[m])
            logit_x[m, x] = jnp.sum(logit_z[m], axis=0)
            for d in range(1, X):
                remote(
                    logit_x.at[m, x], logit_x.at[m, x], lx_send.at[m], lx_recv.at[m],
                    (s, z, xat(d)),
                ).start()
            await_bytes(logit_x.at[m, pl.ds(0, X - 1)], lx_recv.at[m])
            logit_row = jnp.sum(logit_x[m], axis=0)
            lane = lax.broadcasted_iota(jnp.int32, (R, R), 1)
            row = lax.broadcasted_iota(jnp.int32, (R, R), 0)
            sign_row = (2 * labels[pl.ds(m, 1), :] - 1).astype(jnp.float32)
            top_row = -loss_scale * sign_row * jax.nn.sigmoid(-sign_row * logit_row[:, :R])
            top = jnp.sum(
                jnp.where(lane == row, jnp.broadcast_to(top_row, (R, R)), 0.0),
                axis=1, keepdims=True,
            )
            ghid[m] = (top * head[...]).astype(jnp.bfloat16)

        @pl.when(s < S - 1)
        def _():
            await_bytes(col_in.at[m], bz_recv.at[m])
            await_bytes(gh_in.at[m], bg_recv.at[m])
            back = jnp.sum(col_in[m].astype(jnp.float32), axis=0)
            ghid[m] = (gh_in[m].astype(jnp.float32) + back).astype(jnp.bfloat16)

        grad = (ghid[m].astype(jnp.float32) * silu_slope(pre[m])).astype(jnp.bfloat16)
        gpre[m] = grad

        @pl.when(s > 0)
        def _():
            remote(
                ghid.at[m], gh_in.at[m], bg_send.at[m], bg_recv.at[m], (prv, z, x)
            ).start()
            for g, (first, size) in reversed(list(enumerate(groups))):
                slots = pl.ds(first, size)
                for d in [*x_far, 0]:
                    xi = xat(d)
                    for k in range(first, first + size):
                        part[m, xi, k] = lax.dot_general(
                            grad, w[z_slot[k] * X + xi], (((1,), (1,)), ((), ())),
                            preferred_element_type=jnp.float32,
                        ).astype(jnp.bfloat16)
                    if d:
                        remote(
                            part.at[m, xi, slots], part_in.at[m, x, slots], bx_send.at[m],
                            bx_recv.at[m, g], (s, z, xi),
                        ).start()
            for g, (first, size) in reversed(list(enumerate(groups))):
                await_bytes(
                    part_in.at[m, pl.ds(0, X - 1), pl.ds(first, size)], bx_recv.at[m, g]
                )
                order = range(first + size - 1, first - 1, -1)
                for k in order:
                    column_sum = part[m, x, k].astype(jnp.float32)
                    for e in range(1, X):
                        column_sum = column_sum + part_in[m, xat(e), k].astype(jnp.float32)
                    colsum[m, k] = (column_sum * inv_sig[...]).astype(jnp.bfloat16)
                for k in order:
                    remote(
                        colsum.at[m, k], col_in.at[m, z], bz_send.at[m], bz_recv.at[m],
                        (prv, z_slot[k], x),
                    ).start()

        return carry

    @pl.when(s < S - 1)
    def _():
        lax.fori_loop(0, n, forward_micro, 0)
        lax.fori_loop(0, n, backward_micro, 0)

    @pl.when(s == S - 1)
    def _():
        forward_micro(0, 0)

        def turn(m, carry):
            forward_micro(m, carry)
            backward_micro(m - 1, carry)
            return carry

        lax.fori_loop(1, n, turn, 0)
        backward_micro(n - 1, 0)

    inner = jnp.sum(gpre[...].astype(jnp.float32) * pre[...], axis=0)
    coef_z[z] = jnp.sum(inner, axis=0, keepdims=True)
    spread_z(lambda d: coef_z.at[z], coef_z.at[z], 6)

    grads = gpre[...].reshape(n * R, LANES)

    def weight_block(k, zi):
        for xi in range(X):
            rows = hid[:, xi, k].reshape(n * R, LANES)
            block = lax.dot_general(
                rows, grads, (((0,), (0,)), ((), ())), preferred_element_type=jnp.float32
            )
            wg_out[zi * X + xi] = (block * inv_sig[...]).astype(jnp.bfloat16)

    for k in range(Z):
        weight_block(k, z_slot[k])

    await_bytes(coef_z.at[pl.ds(0, Z - 1)], small_recv.at[6])
    coef_x[x] = jnp.sum(coef_z[...], axis=0)
    spread_x(lambda d: coef_x.at[x], coef_x.at[x], 7)
    await_bytes(coef_x.at[pl.ds(0, X - 1)], small_recv.at[7])
    inner_total = jnp.sum(jnp.sum(coef_x[...], axis=0), axis=-1, keepdims=True)
    coef_out[...] = inner_total * inv_sig[...]

    await_bytes(left_xin.at[pl.ds(0, X - 1)], small_send.at[0])
    await_bytes(left_zin.at[pl.ds(0, Z - 1)], small_send.at[1])
    await_bytes(left_xin.at[pl.ds(0, X - 1)], small_send.at[3])
    for k, buf in ((4, norm_z), (6, coef_z)):
        await_bytes(buf.at[pl.ds(0, Z - 1)], small_send.at[k])
    for k, buf in ((5, norm_x), (7, coef_x)):
        await_bytes(buf.at[pl.ds(0, X - 1)], small_send.at[k])

    def drain(m, carry):
        await_bytes(hid.at[m, 0], fz_send.at[m])
        await_bytes(hid.at[m, pl.ds(0, X - 1)], fx_send.at[m])

        @pl.when(s > 0)
        def _():
            await_bytes(ghid.at[m], bg_send.at[m])
            await_bytes(part_in.at[m, pl.ds(0, X - 1)], bx_send.at[m])
            await_bytes(colsum.at[m], bz_send.at[m])

        @pl.when(s == S - 1)
        def _():
            await_bytes(logit_z.at[m, pl.ds(0, Z - 1)], lz_send.at[m])
            await_bytes(logit_x.at[m, pl.ds(0, X - 1)], lx_send.at[m])

        return carry

    lax.fori_loop(0, n, drain, 0)


def on_device(features, labels, weights, vectors, head_weight):
    S, Z, X = lax.axis_size("section"), lax.axis_size("mp_0"), lax.axis_size("mp_1")
    n, R, _ = features.shape
    blocks = Z * X
    bf, f32 = jnp.bfloat16, jnp.float32
    vmem = pl.BlockSpec(memory_space=pltpu.VMEM)
    dma = pltpu.SemaphoreType.DMA
    wg, nu, coef = pl.pallas_call(
        functools.partial(step_kernel, (S, Z, X, n, R)),
        out_shape=(
            jax.ShapeDtypeStruct((blocks, LANES, LANES), bf),
            jax.ShapeDtypeStruct((1, LANES), f32),
            jax.ShapeDtypeStruct((1, LANES), f32),
        ),
        in_specs=[vmem, vmem, pl.BlockSpec(memory_space=pl.ANY), vmem, vmem],
        out_specs=(vmem, vmem, vmem),
        scratch_shapes=[
            pltpu.VMEM((blocks, LANES, LANES), bf),
            dma,
            pltpu.VMEM((n, X, Z, R, LANES), bf),
            pltpu.VMEM((n, R, LANES), bf),
            pltpu.VMEM((n, R, LANES), f32),
            pltpu.VMEM((n, R, LANES), bf),
            pltpu.VMEM((n, R, LANES), bf),
            pltpu.VMEM((n, X, Z, R, LANES), bf),
            pltpu.VMEM((n, X, Z, R, LANES), bf),
            pltpu.VMEM((n, Z, R, LANES), bf),
            pltpu.VMEM((n, Z, R, LANES), bf),
            pltpu.VMEM((n, R, LANES), bf),
            pltpu.VMEM((X, Z, 1, LANES), f32),
            pltpu.VMEM((X, Z, 1, LANES), f32),
            pltpu.VMEM((Z, Z, 1, LANES), f32),
            pltpu.VMEM((X, Z, 1, LANES), f32),
            pltpu.VMEM((Z, 1, LANES), f32),
            pltpu.VMEM((X, 1, LANES), f32),
            pltpu.VMEM((n, Z, 1, LANES), f32),
            pltpu.VMEM((n, X, 1, LANES), f32),
            pltpu.VMEM((Z, 1, LANES), f32),
            pltpu.VMEM((X, 1, LANES), f32),
            pltpu.VMEM((1, LANES), f32),
            dma((8,)),
            dma((8,)),
            dma((n,)),
            dma((n, 3)),
            dma((n,)),
            dma((n, 3)),
            dma((n,)),
            dma((n, 3)),
            dma((n,)),
            dma((n,)),
            dma((n,)),
            dma((n,)),
            dma((n,)),
            dma((n,)),
            dma((n,)),
            dma((n,)),
        ],
        compiler_params=pltpu.CompilerParams(collective_id=0, has_side_effects=True),
    )(
        features,
        labels,
        weights.reshape(blocks, LANES, LANES),
        vectors,
        head_weight[None],
    )
    return wg.reshape(1, blocks * LANES, LANES), nu, coef[0, :1]


def solution(mesh):
    columns = [4 if mesh.shape["mp"] == 64 else 2]
    x_size = columns[0]
    sections = mesh.shape["section"]
    torus = Mesh(
        mesh.devices.reshape(sections, mesh.shape["mp"] // x_size, x_size),
        ("section", "mp_0", "mp_1"),
    )
    placed = (P(None, None, MP), P(), P("section", None, MP), P("section", MP), P(MP))
    return jax.shard_map(
        on_device,
        mesh=torus,
        in_specs=placed,
        out_specs=(P("section", None, MP), P("section", MP), P("section")),
        check_vma=False,
    )
```

```python
import functools

import jax
import jax.numpy as jnp
from jax import lax
from jax.experimental import pallas as pl
from jax.experimental.pallas import tpu as pltpu
from jax.sharding import Mesh
from jax.sharding import PartitionSpec as P

MP = ("mp_0", "mp_1")
loss_scale = 32.0
tiny_eps = 1e-06
LANES = 128


def silu_slope(pre_act):
    gate_val = jax.nn.sigmoid(pre_act)
    return gate_val * (1.0 + pre_act * (1.0 - gate_val))


def near_first(count):
    return sorted(range(count), key=lambda d: min(d, count - d))


def remote(src, dst, send, recv, device):
    return pltpu.make_async_remote_copy(
        src_ref=src,
        dst_ref=dst,
        send_sem=send,
        recv_sem=recv,
        device_id=device,
        device_id_type=pl.DeviceIdType.MESH,
    )


def await_bytes(ref, sem):
    pltpu.make_async_copy(ref, ref, sem).wait()


def step_kernel(
    dims,
    feat,
    labels,
    w_hbm,
    u,
    head,
    wg_out,
    nu_out,
    coef_out,
    w,
    w_sem,
    hid,
    hout,
    pre,
    gpre,
    ghid,
    part,
    part_in,
    colsum,
    col_in,
    gh_in,
    left_x,
    left_xin,
    left_zin,
    left_all,
    norms,
    logits,
    coefs,
    inv_sig,
    small_send,
    small_recv,
    fz_send,
    fz_recv,
    fx_send,
    fx_recv,
    bx_send,
    bx_recv,
    bz_send,
    bz_recv,
    bg_send,
    bg_recv,
    lz_send,
    lz_recv,
):
    S, Z, X, n, R = dims
    near = near_first(Z)
    z_far = near[::-1]
    slot_of = {d: k for k, d in enumerate(near)}
    groups = [(0, Z // 2), (Z // 2, Z // 4), (Z // 2 + Z // 4, Z // 4)]
    group_of = [0] * (Z // 2) + [1] * (Z // 4) + [2] * (Z // 4)
    s = lax.axis_index("section")
    z = lax.axis_index("mp_0")
    x = lax.axis_index("mp_1")
    nxt = lax.rem(s + 1, S)
    prv = lax.rem(s + S - 1, S)
    x_far = near_first(X)[:0:-1]

    peers = [(d, e) for d in z_far for e in range(X) if d or e]
    me = z * X + x

    def zat(d):
        return lax.rem(z + d, Z)

    def xat(d):
        return lax.rem(x + d, X)

    barrier = pltpu.get_barrier_semaphore()

    def greet(device):
        pl.semaphore_signal(
            barrier, inc=1, device_id=device, device_id_type=pl.DeviceIdType.MESH
        )

    for d in z_far:
        greet((nxt, zat(d), x))
        greet((prv, zat(d), x))
    for d, e in peers:
        greet((s, zat(d), xat(e)))

    load_w = pltpu.make_async_copy(w_hbm, w, w_sem)
    load_w.start()
    z_slot = [zat(d) for d in near]
    u_rows = jnp.broadcast_to(u[...], (16, LANES)).astype(jnp.bfloat16)

    def left_block(zi, carry):
        for xi in range(X):
            block = lax.dot_general(
                u_rows, w[zi * X + xi], (((1,), (1,)), ((), ())),
                preferred_element_type=jnp.float32,
            )
            left_x[xi, zi] = block[0:1]
        return carry

    load_w.wait()
    lax.fori_loop(0, Z, left_block, 0)
    pl.semaphore_wait(barrier, 2 * Z + len(peers))

    @pl.when(s == S - 1)
    def _():
        def send_features(m, carry):
            for d in z_far:
                k = slot_of[(Z - d) % Z]
                remote(
                    feat.at[m], hid.at[m, x, k], fz_send.at[m], fz_recv.at[m, group_of[k]],
                    (nxt, zat(d), x),
                ).start()
            return carry

        lax.fori_loop(0, n, send_features, 0)

    def spread_z(src, dst, k):
        for d in z_far:
            if d:
                remote(src(d), dst, small_send.at[k], small_recv.at[k], (s, zat(d), x)).start()

    def share(row, send, recv):
        for d, e in peers:
            remote(row, row, send, recv, (s, zat(d), xat(e))).start()

    def spread_x(src, dst, k):
        for d in range(1, X):
            remote(src(d), dst, small_send.at[k], small_recv.at[k], (s, z, xat(d))).start()

    spread_x(lambda d: left_x.at[xat(d)], left_xin.at[x], 0)
    await_bytes(left_xin.at[pl.ds(0, X - 1)], small_recv.at[0])
    column = left_x[x]
    for d in range(1, X):
        column = column + left_xin[xat(d)]
    left_zin[z] = column
    spread_z(lambda d: left_zin.at[z], left_zin.at[z], 1)

    def forward_columns(m):
        for g, (first, size) in enumerate(groups):
            slots = pl.ds(first, size)
            await_bytes(hid.at[m, x, slots], fz_recv.at[m, g])
            for d in x_far:
                remote(
                    hid.at[m, x, slots], hid.at[m, x, slots], fx_send.at[m], fx_recv.at[m, g],
                    (s, z, xat(d)),
                ).start()

    await_bytes(left_zin.at[pl.ds(0, Z - 1)], small_recv.at[1])
    left_all[x] = jnp.sum(left_zin[...], axis=0)
    spread_x(lambda d: left_all.at[x], left_all.at[x], 3)
    await_bytes(left_all.at[pl.ds(0, X - 1)], small_recv.at[3])

    left = left_all[...]
    total = jnp.sum(jnp.sum(left * left, axis=(0, 1)), axis=-1, keepdims=True)
    scale_v = lax.rsqrt(total + tiny_eps)

    def pair(ref_rows):
        return jnp.concatenate(ref_rows, axis=1)

    def w_pair(xi, zi):
        return jnp.concatenate([w[zi * X + xi], w[(zi + 1) * X + xi]], axis=0)

    def right_block(zp, acc):
        zi = zp * 2
        for xi in range(X):
            rows = [
                jnp.broadcast_to(left_all[xi, zi + k] * scale_v, (16, LANES)).astype(jnp.bfloat16)
                for k in range(2)
            ]
            acc = acc + jnp.dot(pair(rows), w_pair(xi, zi), preferred_element_type=jnp.float32)
        return acc

    right = lax.fori_loop(0, Z // 2, right_block, jnp.zeros((16, LANES), jnp.float32))[0:1]

    norms[me] = right * right
    share(norms.at[me], small_send.at[4], small_recv.at[4])

    @pl.when(s == 0)
    def _():
        def pass_on(m, carry):
            forward_columns(m)
            return carry

        lax.fori_loop(0, n, pass_on, 0)

    await_bytes(norms.at[pl.ds(0, Z * X - 1)], small_recv.at[4])
    norm_total = jnp.sum(jnp.sum(norms[...], axis=0), axis=-1, keepdims=True)
    inv = 1.0 / jnp.sqrt(norm_total + tiny_eps)
    inv_sig[...] = jnp.broadcast_to(inv, (1, LANES))
    nu_out[...] = right * inv

    def forward_start(m):
        @pl.when(s > 0)
        def _():
            forward_columns(m)

    def forward_end(m):
        def partial_dots(acc, d, first, size):
            xi = xat(d)
            for k in range(first, first + size, 2):
                rows = jnp.concatenate([hid[m, xi, k], hid[m, xi, k + 1]], axis=1)
                cols = jnp.concatenate(
                    [w[z_slot[k] * X + xi], w[z_slot[k + 1] * X + xi]], axis=0
                )
                acc = acc + jnp.dot(rows, cols, preferred_element_type=jnp.float32)
            return acc

        acc = partial_dots(jnp.zeros((R, LANES), jnp.float32), 0, 0, Z)
        for g, (first, size) in enumerate(groups):
            await_bytes(hid.at[m, pl.ds(0, X - 1), pl.ds(first, size)], fx_recv.at[m, g])
            for d in range(1, X):
                acc = partial_dots(acc, d, first, size)
        pre_act = acc * inv_sig[...]
        pre[m] = pre_act
        out = (hid[m, x, 0].astype(jnp.float32) + pre_act * jax.nn.sigmoid(pre_act)).astype(
            jnp.bfloat16
        )
        hout[m] = out

        @pl.when(s < S - 1)
        def _():
            for d in z_far:
                k = slot_of[(Z - d) % Z]
                remote(
                    hout.at[m], hid.at[m, x, k], fz_send.at[m], fz_recv.at[m, group_of[k]],
                    (nxt, zat(d), x),
                ).start()

        @pl.when(s == S - 1)
        def _():
            terms = jnp.sum(out.astype(jnp.float32) * head[...], axis=1, keepdims=True)
            lane = lax.broadcasted_iota(jnp.int32, (R, LANES), 1)
            row = lax.broadcasted_iota(jnp.int32, (R, LANES), 0)
            spread = jnp.where(lane == row, jnp.broadcast_to(terms, (R, LANES)), 0.0)
            logits[m, me] = jnp.sum(spread, axis=0, keepdims=True)
            share(logits.at[m, me], lz_send.at[m], lz_recv.at[m])

    def backward_start(m):
        @pl.when(s == S - 1)
        def _():
            await_bytes(logits.at[m, pl.ds(0, Z * X - 1)], lz_recv.at[m])
            logit_row = jnp.sum(logits[m], axis=0)
            lane = lax.broadcasted_iota(jnp.int32, (R, R), 1)
            row = lax.broadcasted_iota(jnp.int32, (R, R), 0)
            sign_row = (2 * labels[pl.ds(m, 1), :] - 1).astype(jnp.float32)
            top_row = -loss_scale * sign_row * jax.nn.sigmoid(-sign_row * logit_row[:, :R])
            top = jnp.sum(
                jnp.where(lane == row, jnp.broadcast_to(top_row, (R, R)), 0.0),
                axis=1, keepdims=True,
            )
            ghid[m] = (top * head[...]).astype(jnp.bfloat16)

        @pl.when(s < S - 1)
        def _():
            await_bytes(col_in.at[m], bz_recv.at[m])
            await_bytes(gh_in.at[m], bg_recv.at[m])
            back = jnp.sum(col_in[m].astype(jnp.float32), axis=0)
            ghid[m] = (gh_in[m].astype(jnp.float32) + back).astype(jnp.bfloat16)

        grad = (ghid[m].astype(jnp.float32) * silu_slope(pre[m])).astype(jnp.bfloat16)
        gpre[m] = grad

        @pl.when(s > 0)
        def _():
            remote(
                ghid.at[m], gh_in.at[m], bg_send.at[m], bg_recv.at[m], (prv, z, x)
            ).start()
            for g, (first, size) in reversed(list(enumerate(groups))):
                slots = pl.ds(first, size)
                for d in [*x_far, 0]:
                    xi = xat(d)
                    for k in range(first, first + size):
                        part[m, xi, k] = lax.dot_general(
                            grad, w[z_slot[k] * X + xi], (((1,), (1,)), ((), ())),
                            preferred_element_type=jnp.float32,
                        ).astype(jnp.bfloat16)
                    if d:
                        remote(
                            part.at[m, xi, slots], part_in.at[m, x, slots], bx_send.at[m],
                            bx_recv.at[m, g], (s, z, xi),
                        ).start()

    def backward_end(m):
        @pl.when(s > 0)
        def _():
            for g, (first, size) in reversed(list(enumerate(groups))):
                await_bytes(
                    part_in.at[m, pl.ds(0, X - 1), pl.ds(first, size)], bx_recv.at[m, g]
                )
                order = range(first + size - 1, first - 1, -1)
                for k in order:
                    column_sum = part[m, x, k].astype(jnp.float32)
                    for e in range(1, X):
                        column_sum = column_sum + part_in[m, xat(e), k].astype(jnp.float32)
                    colsum[m, k] = (column_sum * inv_sig[...]).astype(jnp.bfloat16)
                for k in order:
                    remote(
                        colsum.at[m, k], col_in.at[m, z], bz_send.at[m], bz_recv.at[m],
                        (prv, z_slot[k], x),
                    ).start()

    def forward_turn(m, carry):
        forward_start(m + 1)
        forward_end(m)
        return carry

    def backward_turn(m, carry):
        backward_start(m + 1)
        backward_end(m)
        return carry

    forward_start(0)
    lax.fori_loop(0, n - 1, forward_turn, 0)

    @pl.when(s == S - 1)
    def _():
        backward_start(0)

    forward_end(n - 1)

    @pl.when(s < S - 1)
    def _():
        backward_start(0)

    lax.fori_loop(0, n - 1, backward_turn, 0)
    backward_end(n - 1)

    inner = jnp.sum(gpre[...].astype(jnp.float32) * pre[...], axis=0)
    coefs[me] = jnp.sum(inner, axis=0, keepdims=True)
    share(coefs.at[me], small_send.at[6], small_recv.at[6])

    grads = gpre[...].reshape(n * R, LANES)

    def weight_block(k, zi):
        for xi in range(X):
            rows = hid[:, xi, k].reshape(n * R, LANES)
            block = lax.dot_general(
                rows, grads, (((0,), (0,)), ((), ())), preferred_element_type=jnp.float32
            )
            wg_out[zi * X + xi] = (block * inv_sig[...]).astype(jnp.bfloat16)

    for k in range(Z):
        weight_block(k, z_slot[k])

    await_bytes(coefs.at[pl.ds(0, Z * X - 1)], small_recv.at[6])
    inner_total = jnp.sum(jnp.sum(coefs[...], axis=0), axis=-1, keepdims=True)
    coef_out[...] = inner_total * inv_sig[...]

    await_bytes(left_xin.at[pl.ds(0, X - 1)], small_send.at[0])
    await_bytes(left_zin.at[pl.ds(0, Z - 1)], small_send.at[1])
    await_bytes(left_xin.at[pl.ds(0, X - 1)], small_send.at[3])
    await_bytes(norms.at[pl.ds(0, Z * X - 1)], small_send.at[4])
    await_bytes(coefs.at[pl.ds(0, Z * X - 1)], small_send.at[6])

    def drain(m, carry):
        await_bytes(hid.at[m, 0], fz_send.at[m])
        await_bytes(hid.at[m, pl.ds(0, X - 1)], fx_send.at[m])

        @pl.when(s > 0)
        def _():
            await_bytes(ghid.at[m], bg_send.at[m])
            await_bytes(part_in.at[m, pl.ds(0, X - 1)], bx_send.at[m])
            await_bytes(colsum.at[m], bz_send.at[m])

        @pl.when(s == S - 1)
        def _():
            await_bytes(logits.at[m, pl.ds(0, Z * X - 1)], lz_send.at[m])

        return carry

    lax.fori_loop(0, n, drain, 0)


def on_device(features, labels, weights, vectors, head_weight):
    S, Z, X = lax.axis_size("section"), lax.axis_size("mp_0"), lax.axis_size("mp_1")
    n, R, _ = features.shape
    blocks = Z * X
    bf, f32 = jnp.bfloat16, jnp.float32
    vmem = pl.BlockSpec(memory_space=pltpu.VMEM)
    dma = pltpu.SemaphoreType.DMA
    wg, nu, coef = pl.pallas_call(
        functools.partial(step_kernel, (S, Z, X, n, R)),
        out_shape=(
            jax.ShapeDtypeStruct((blocks, LANES, LANES), bf),
            jax.ShapeDtypeStruct((1, LANES), f32),
            jax.ShapeDtypeStruct((1, LANES), f32),
        ),
        in_specs=[vmem, vmem, pl.BlockSpec(memory_space=pl.ANY), vmem, vmem],
        out_specs=(vmem, vmem, vmem),
        scratch_shapes=[
            pltpu.VMEM((blocks, LANES, LANES), bf),
            dma,
            pltpu.VMEM((n, X, Z, R, LANES), bf),
            pltpu.VMEM((n, R, LANES), bf),
            pltpu.VMEM((n, R, LANES), f32),
            pltpu.VMEM((n, R, LANES), bf),
            pltpu.VMEM((n, R, LANES), bf),
            pltpu.VMEM((n, X, Z, R, LANES), bf),
            pltpu.VMEM((n, X, Z, R, LANES), bf),
            pltpu.VMEM((n, Z, R, LANES), bf),
            pltpu.VMEM((n, Z, R, LANES), bf),
            pltpu.VMEM((n, R, LANES), bf),
            pltpu.VMEM((X, Z, 1, LANES), f32),
            pltpu.VMEM((X, Z, 1, LANES), f32),
            pltpu.VMEM((Z, Z, 1, LANES), f32),
            pltpu.VMEM((X, Z, 1, LANES), f32),
            pltpu.VMEM((blocks, 1, LANES), f32),
            pltpu.VMEM((n, blocks, 1, LANES), f32),
            pltpu.VMEM((blocks, 1, LANES), f32),
            pltpu.VMEM((1, LANES), f32),
            dma((8,)),
            dma((8,)),
            dma((n,)),
            dma((n, 3)),
            dma((n,)),
            dma((n, 3)),
            dma((n,)),
            dma((n, 3)),
            dma((n,)),
            dma((n,)),
            dma((n,)),
            dma((n,)),
            dma((n,)),
            dma((n,)),
        ],
        compiler_params=pltpu.CompilerParams(collective_id=0, has_side_effects=True),
    )(
        features,
        labels,
        weights.reshape(blocks, LANES, LANES),
        vectors,
        head_weight[None],
    )
    return wg.reshape(1, blocks * LANES, LANES), nu, coef[0, :1]


def solution(mesh):
    columns = [4 if mesh.shape["mp"] == 64 else 2]
    x_size = columns[0]
    sections = mesh.shape["section"]
    torus = Mesh(
        mesh.devices.reshape(sections, mesh.shape["mp"] // x_size, x_size),
        ("section", "mp_0", "mp_1"),
    )
    placed = (P(None, None, MP), P(), P("section", None, MP), P("section", MP), P(MP))
    return jax.shard_map(
        on_device,
        mesh=torus,
        in_specs=placed,
        out_specs=(P("section", None, MP), P("section", MP), P("section")),
        check_vma=False,
    )
```

```python
import functools

import jax
import jax.numpy as jnp
from jax import lax
from jax.experimental import pallas as pl
from jax.experimental.pallas import tpu as pltpu
from jax.sharding import Mesh
from jax.sharding import PartitionSpec as P

MP = ("mp_0", "mp_1")
loss_scale = 32.0
tiny_eps = 1e-06
LANES = 128


def silu_slope(pre_act):
    gate_val = jax.nn.sigmoid(pre_act)
    return gate_val * (1.0 + pre_act * (1.0 - gate_val))


def near_first(count):
    return sorted(range(count), key=lambda d: min(d, count - d))


def remote(src, dst, send, recv, device):
    return pltpu.make_async_remote_copy(
        src_ref=src,
        dst_ref=dst,
        send_sem=send,
        recv_sem=recv,
        device_id=device,
        device_id_type=pl.DeviceIdType.MESH,
    )


def await_bytes(ref, sem):
    pltpu.make_async_copy(ref, ref, sem).wait()


def step_kernel(
    dims,
    feat,
    labels,
    w_hbm,
    u,
    head,
    wg_out,
    nu_out,
    coef_out,
    w,
    w_sem,
    hid,
    hout,
    pre,
    gpre,
    ghid,
    part,
    part_in,
    colsum,
    col_in,
    gh_in,
    left_x,
    left_xin,
    left_zin,
    left_all,
    norms,
    logits,
    coefs,
    inv_sig,
    small_send,
    small_recv,
    fz_send,
    fz_recv,
    fx_send,
    fx_recv,
    bx_send,
    bx_recv,
    bz_send,
    bz_recv,
    bg_send,
    bg_recv,
    lz_send,
    lz_recv,
):
    S, Z, X, n, R = dims
    near = near_first(Z)
    z_far = near[::-1]
    slot_of = {d: k for k, d in enumerate(near)}
    groups = [(0, Z // 2), (Z // 2, Z // 4), (Z // 2 + Z // 4, Z // 4)]
    group_of = [0] * (Z // 2) + [1] * (Z // 4) + [2] * (Z // 4)
    s = lax.axis_index("section")
    z = lax.axis_index("mp_0")
    x = lax.axis_index("mp_1")
    nxt = lax.rem(s + 1, S)
    prv = lax.rem(s + S - 1, S)
    x_far = near_first(X)[:0:-1]

    peers = [(d, e) for d in z_far for e in range(X) if d or e]
    me = z * X + x

    def zat(d):
        return lax.rem(z + d, Z)

    def xat(d):
        return lax.rem(x + d, X)

    barrier = pltpu.get_barrier_semaphore()

    def greet(device):
        pl.semaphore_signal(
            barrier, inc=1, device_id=device, device_id_type=pl.DeviceIdType.MESH
        )

    for d in z_far:
        greet((nxt, zat(d), x))
        greet((prv, zat(d), x))
    for d, e in peers:
        greet((s, zat(d), xat(e)))

    load_w = pltpu.make_async_copy(w_hbm, w, w_sem)
    load_w.start()
    z_slot = [zat(d) for d in near]
    u_rows = jnp.broadcast_to(u[...], (16, LANES)).astype(jnp.bfloat16)

    def left_block(zi, carry):
        for xi in range(X):
            block = lax.dot_general(
                u_rows, w[zi * X + xi], (((1,), (1,)), ((), ())),
                preferred_element_type=jnp.float32,
            )
            left_x[xi, zi] = block[0:1]
        return carry

    load_w.wait()
    lax.fori_loop(0, Z, left_block, 0)
    pl.semaphore_wait(barrier, 2 * Z + len(peers))

    @pl.when(s == S - 1)
    def _():
        def send_features(m, carry):
            for d in z_far:
                k = slot_of[(Z - d) % Z]
                remote(
                    feat.at[m], hid.at[m, x, k], fz_send.at[m], fz_recv.at[m, group_of[k]],
                    (nxt, zat(d), x),
                ).start()
            return carry

        lax.fori_loop(0, n, send_features, 0)

    def spread_z(src, dst, k):
        for d in z_far:
            if d:
                remote(src(d), dst, small_send.at[k], small_recv.at[k], (s, zat(d), x)).start()

    def share(row, send, recv):
        for d, e in peers:
            remote(row, row, send, recv, (s, zat(d), xat(e))).start()

    def spread_x(src, dst, k):
        for d in range(1, X):
            remote(src(d), dst, small_send.at[k], small_recv.at[k], (s, z, xat(d))).start()

    spread_x(lambda d: left_x.at[xat(d)], left_xin.at[x], 0)
    await_bytes(left_xin.at[pl.ds(0, X - 1)], small_recv.at[0])
    column = left_x[x]
    for d in range(1, X):
        column = column + left_xin[xat(d)]
    left_zin[z] = column
    spread_z(lambda d: left_zin.at[z], left_zin.at[z], 1)

    def forward_columns(m):
        for g, (first, size) in enumerate(groups):
            slots = pl.ds(first, size)
            await_bytes(hid.at[m, x, slots], fz_recv.at[m, g])
            for d in x_far:
                remote(
                    hid.at[m, x, slots], hid.at[m, x, slots], fx_send.at[m], fx_recv.at[m, g],
                    (s, z, xat(d)),
                ).start()

    await_bytes(left_zin.at[pl.ds(0, Z - 1)], small_recv.at[1])
    left_all[x] = jnp.sum(left_zin[...], axis=0)
    spread_x(lambda d: left_all.at[x], left_all.at[x], 3)
    await_bytes(left_all.at[pl.ds(0, X - 1)], small_recv.at[3])

    left = left_all[...]
    total = jnp.sum(jnp.sum(left * left, axis=(0, 1)), axis=-1, keepdims=True)
    scale_v = lax.rsqrt(total + tiny_eps)

    def pair(ref_rows):
        return jnp.concatenate(ref_rows, axis=1)

    def w_pair(xi, zi):
        return jnp.concatenate([w[zi * X + xi], w[(zi + 1) * X + xi]], axis=0)

    def right_block(zp, acc):
        zi = zp * 2
        for xi in range(X):
            rows = [
                jnp.broadcast_to(left_all[xi, zi + k] * scale_v, (16, LANES)).astype(jnp.bfloat16)
                for k in range(2)
            ]
            acc = acc + jnp.dot(pair(rows), w_pair(xi, zi), preferred_element_type=jnp.float32)
        return acc

    right = lax.fori_loop(0, Z // 2, right_block, jnp.zeros((16, LANES), jnp.float32))[0:1]

    norms[me] = right * right
    share(norms.at[me], small_send.at[4], small_recv.at[4])

    @pl.when(s == 0)
    def _():
        def pass_on(m, carry):
            forward_columns(m)
            return carry

        lax.fori_loop(0, n, pass_on, 0)

    await_bytes(norms.at[pl.ds(0, Z * X - 1)], small_recv.at[4])
    norm_total = jnp.sum(jnp.sum(norms[...], axis=0), axis=-1, keepdims=True)
    inv = 1.0 / jnp.sqrt(norm_total + tiny_eps)
    inv_sig[...] = jnp.broadcast_to(inv, (1, LANES))
    nu_out[...] = right * inv

    def forward_start(m):
        @pl.when(s > 0)
        def _():
            forward_columns(m)

    def forward_end(m):
        def partial_dots(acc, d, first, size):
            xi = xat(d)
            for k in range(first, first + size, 2):
                rows = jnp.concatenate([hid[m, xi, k], hid[m, xi, k + 1]], axis=1)
                cols = jnp.concatenate(
                    [w[z_slot[k] * X + xi], w[z_slot[k + 1] * X + xi]], axis=0
                )
                acc = acc + jnp.dot(rows, cols, preferred_element_type=jnp.float32)
            return acc

        acc = partial_dots(jnp.zeros((R, LANES), jnp.float32), 0, 0, Z)
        for g, (first, size) in enumerate(groups):
            await_bytes(hid.at[m, pl.ds(0, X - 1), pl.ds(first, size)], fx_recv.at[m, g])
            for d in range(1, X):
                acc = partial_dots(acc, d, first, size)
        pre_act = acc * inv_sig[...]
        pre[m] = pre_act
        out = (hid[m, x, 0].astype(jnp.float32) + pre_act * jax.nn.sigmoid(pre_act)).astype(
            jnp.bfloat16
        )
        hout[m] = out

        @pl.when(s < S - 1)
        def _():
            for d in z_far:
                k = slot_of[(Z - d) % Z]
                remote(
                    hout.at[m], hid.at[m, x, k], fz_send.at[m], fz_recv.at[m, group_of[k]],
                    (nxt, zat(d), x),
                ).start()

        @pl.when(s == S - 1)
        def _():
            terms = jnp.sum(out.astype(jnp.float32) * head[...], axis=1, keepdims=True)
            lane = lax.broadcasted_iota(jnp.int32, (R, LANES), 1)
            row = lax.broadcasted_iota(jnp.int32, (R, LANES), 0)
            spread = jnp.where(lane == row, jnp.broadcast_to(terms, (R, LANES)), 0.0)
            logits[m, me] = jnp.sum(spread, axis=0, keepdims=True)
            share(logits.at[m, me], lz_send.at[m], lz_recv.at[m])

    def backward_start(m):
        @pl.when(s == S - 1)
        def _():
            await_bytes(logits.at[m, pl.ds(0, Z * X - 1)], lz_recv.at[m])
            logit_row = jnp.sum(logits[m], axis=0)
            lane = lax.broadcasted_iota(jnp.int32, (R, R), 1)
            row = lax.broadcasted_iota(jnp.int32, (R, R), 0)
            sign_row = (2 * labels[pl.ds(m, 1), :] - 1).astype(jnp.float32)
            top_row = -loss_scale * sign_row * jax.nn.sigmoid(-sign_row * logit_row[:, :R])
            top = jnp.sum(
                jnp.where(lane == row, jnp.broadcast_to(top_row, (R, R)), 0.0),
                axis=1, keepdims=True,
            )
            ghid[m] = (top * head[...]).astype(jnp.bfloat16)

        @pl.when(s < S - 1)
        def _():
            await_bytes(col_in.at[m], bz_recv.at[m])
            await_bytes(gh_in.at[m], bg_recv.at[m])
            back = jnp.sum(col_in[m].astype(jnp.float32), axis=0)
            ghid[m] = (gh_in[m].astype(jnp.float32) + back).astype(jnp.bfloat16)

        grad = (ghid[m].astype(jnp.float32) * silu_slope(pre[m])).astype(jnp.bfloat16)
        gpre[m] = grad

        @pl.when(s > 0)
        def _():
            remote(
                ghid.at[m], gh_in.at[m], bg_send.at[m], bg_recv.at[m], (prv, z, x)
            ).start()
            for g, (first, size) in reversed(list(enumerate(groups))):
                slots = pl.ds(first, size)
                for d in [*x_far, 0]:
                    xi = xat(d)
                    for k in range(first, first + size):
                        part[m, xi, k] = lax.dot_general(
                            grad, w[z_slot[k] * X + xi], (((1,), (1,)), ((), ())),
                            preferred_element_type=jnp.float32,
                        ).astype(jnp.bfloat16)
                    if d:
                        remote(
                            part.at[m, xi, slots], part_in.at[m, x, slots], bx_send.at[m],
                            bx_recv.at[m, g], (s, z, xi),
                        ).start()

    def backward_end(m):
        @pl.when(s > 0)
        def _():
            for g, (first, size) in reversed(list(enumerate(groups))):
                await_bytes(
                    part_in.at[m, pl.ds(0, X - 1), pl.ds(first, size)], bx_recv.at[m, g]
                )
                order = range(first + size - 1, first - 1, -1)
                for k in order:
                    column_sum = part[m, x, k].astype(jnp.float32)
                    for e in range(1, X):
                        column_sum = column_sum + part_in[m, xat(e), k].astype(jnp.float32)
                    colsum[m, k] = (column_sum * inv_sig[...]).astype(jnp.bfloat16)
                for k in order:
                    remote(
                        colsum.at[m, k], col_in.at[m, z], bz_send.at[m], bz_recv.at[m],
                        (prv, z_slot[k], x),
                    ).start()

    turns_apart = jnp.where(s == S - 1, min(3, n), n)

    def turn(t, carry):
        back = t - turns_apart

        @pl.when(t + 1 < n)
        def _():
            forward_start(t + 1)

        @pl.when((back >= 0) & (back < n))
        def _():
            backward_start(back)

        @pl.when(t < n)
        def _():
            forward_end(t)

        @pl.when((back >= 1) & (back <= n))
        def _():
            backward_end(back - 1)

        return carry

    forward_start(0)
    lax.fori_loop(0, 2 * n + 1, turn, 0)

    inner = jnp.sum(gpre[...].astype(jnp.float32) * pre[...], axis=0)
    coefs[me] = jnp.sum(inner, axis=0, keepdims=True)
    share(coefs.at[me], small_send.at[6], small_recv.at[6])

    grads = gpre[...].reshape(n * R, LANES)

    def weight_block(k, zi):
        for xi in range(X):
            rows = hid[:, xi, k].reshape(n * R, LANES)
            block = lax.dot_general(
                rows, grads, (((0,), (0,)), ((), ())), preferred_element_type=jnp.float32
            )
            wg_out[zi * X + xi] = (block * inv_sig[...]).astype(jnp.bfloat16)

    for k in range(Z):
        weight_block(k, z_slot[k])

    await_bytes(coefs.at[pl.ds(0, Z * X - 1)], small_recv.at[6])
    inner_total = jnp.sum(jnp.sum(coefs[...], axis=0), axis=-1, keepdims=True)
    coef_out[...] = inner_total * inv_sig[...]

    await_bytes(left_xin.at[pl.ds(0, X - 1)], small_send.at[0])
    await_bytes(left_zin.at[pl.ds(0, Z - 1)], small_send.at[1])
    await_bytes(left_xin.at[pl.ds(0, X - 1)], small_send.at[3])
    await_bytes(norms.at[pl.ds(0, Z * X - 1)], small_send.at[4])
    await_bytes(coefs.at[pl.ds(0, Z * X - 1)], small_send.at[6])

    def drain(m, carry):
        await_bytes(hid.at[m, 0], fz_send.at[m])
        await_bytes(hid.at[m, pl.ds(0, X - 1)], fx_send.at[m])

        @pl.when(s > 0)
        def _():
            await_bytes(ghid.at[m], bg_send.at[m])
            await_bytes(part_in.at[m, pl.ds(0, X - 1)], bx_send.at[m])
            await_bytes(colsum.at[m], bz_send.at[m])

        @pl.when(s == S - 1)
        def _():
            await_bytes(logits.at[m, pl.ds(0, Z * X - 1)], lz_send.at[m])

        return carry

    lax.fori_loop(0, n, drain, 0)


def on_device(features, labels, weights, vectors, head_weight):
    S, Z, X = lax.axis_size("section"), lax.axis_size("mp_0"), lax.axis_size("mp_1")
    n, R, _ = features.shape
    features = features.reshape(n * 2, R // 2, LANES)
    labels = labels.reshape(n * 2, R // 2)
    n, R = n * 2, R // 2
    blocks = Z * X
    bf, f32 = jnp.bfloat16, jnp.float32
    vmem = pl.BlockSpec(memory_space=pltpu.VMEM)
    dma = pltpu.SemaphoreType.DMA
    wg, nu, coef = pl.pallas_call(
        functools.partial(step_kernel, (S, Z, X, n, R)),
        out_shape=(
            pltpu.VMEM((blocks, LANES, LANES), bf),
            pltpu.VMEM((1, LANES), f32),
            pltpu.VMEM((1, LANES), f32),
        ),
        in_specs=[vmem, vmem, pl.BlockSpec(memory_space=pl.ANY), vmem, vmem],
        out_specs=(vmem, vmem, vmem),
        scratch_shapes=[
            pltpu.VMEM((blocks, LANES, LANES), bf),
            dma,
            pltpu.VMEM((n, X, Z, R, LANES), bf),
            pltpu.VMEM((n, R, LANES), bf),
            pltpu.VMEM((n, R, LANES), f32),
            pltpu.VMEM((n, R, LANES), bf),
            pltpu.VMEM((n, R, LANES), bf),
            pltpu.VMEM((n, X, Z, R, LANES), bf),
            pltpu.VMEM((n, X, Z, R, LANES), bf),
            pltpu.VMEM((n, Z, R, LANES), bf),
            pltpu.VMEM((n, Z, R, LANES), bf),
            pltpu.VMEM((n, R, LANES), bf),
            pltpu.VMEM((X, Z, 1, LANES), f32),
            pltpu.VMEM((X, Z, 1, LANES), f32),
            pltpu.VMEM((Z, Z, 1, LANES), f32),
            pltpu.VMEM((X, Z, 1, LANES), f32),
            pltpu.VMEM((blocks, 1, LANES), f32),
            pltpu.VMEM((n, blocks, 1, LANES), f32),
            pltpu.VMEM((blocks, 1, LANES), f32),
            pltpu.VMEM((1, LANES), f32),
            dma((8,)),
            dma((8,)),
            dma((n,)),
            dma((n, 3)),
            dma((n,)),
            dma((n, 3)),
            dma((n,)),
            dma((n, 3)),
            dma((n,)),
            dma((n,)),
            dma((n,)),
            dma((n,)),
            dma((n,)),
            dma((n,)),
        ],
        compiler_params=pltpu.CompilerParams(collective_id=0, has_side_effects=True),
    )(
        features,
        labels,
        weights.reshape(blocks, LANES, LANES),
        vectors,
        head_weight[None],
    )
    return wg.reshape(1, blocks * LANES, LANES), nu, coef[0, :1]


def solution(mesh):
    columns = [4 if mesh.shape["mp"] == 64 else 2]
    x_size = columns[0]
    sections = mesh.shape["section"]
    torus = Mesh(
        mesh.devices.reshape(sections, mesh.shape["mp"] // x_size, x_size),
        ("section", "mp_0", "mp_1"),
    )
    placed = (P(None, None, MP), P(), P("section", None, MP), P("section", MP), P(MP))
    return jax.shard_map(
        on_device,
        mesh=torus,
        in_specs=placed,
        out_specs=(P("section", None, MP), P("section", MP), P("section")),
        check_vma=False,
    )
```

```python
import functools

import jax
import jax.numpy as jnp
from jax import lax
from jax.experimental import pallas as pl
from jax.experimental.pallas import tpu as pltpu
from jax.sharding import Mesh
from jax.sharding import PartitionSpec as P

MP = ("mp_0", "mp_1")
loss_scale = 32.0
tiny_eps = 1e-06
LANES = 128


def silu_slope(pre_act):
    gate_val = jax.nn.sigmoid(pre_act)
    return gate_val * (1.0 + pre_act * (1.0 - gate_val))


def near_first(count):
    return sorted(range(count), key=lambda d: min(d, count - d))


def remote(src, dst, send, recv, device):
    return pltpu.make_async_remote_copy(
        src_ref=src,
        dst_ref=dst,
        send_sem=send,
        recv_sem=recv,
        device_id=device,
        device_id_type=pl.DeviceIdType.MESH,
    )


def await_bytes(ref, sem):
    pltpu.make_async_copy(ref, ref, sem).wait()


def step_kernel(
    dims,
    feat,
    labels,
    w_hbm,
    u,
    head,
    wg_out,
    nu_out,
    coef_out,
    w,
    w_turned,
    w_sem,
    hid,
    hout,
    pre,
    gpre,
    ghid,
    part,
    part_in,
    colsum,
    col_in,
    gh_in,
    left_x,
    left_xin,
    left_zin,
    left_all,
    norms,
    logits,
    coefs,
    inv_sig,
    small_send,
    small_recv,
    fz_send,
    fz_recv,
    fx_send,
    fx_recv,
    bx_send,
    bx_recv,
    bz_send,
    bz_recv,
    bg_send,
    bg_recv,
    lz_send,
    lz_recv,
):
    S, Z, X, n, R = dims
    near = near_first(Z)
    z_far = near[::-1]
    slot_of = {d: k for k, d in enumerate(near)}
    groups = [(0, Z // 2), (Z // 2, Z // 4), (Z // 2 + Z // 4, Z // 4)]
    group_of = [0] * (Z // 2) + [1] * (Z // 4) + [2] * (Z // 4)
    s = lax.axis_index("section")
    z = lax.axis_index("mp_0")
    x = lax.axis_index("mp_1")
    nxt = lax.rem(s + 1, S)
    prv = lax.rem(s + S - 1, S)
    x_far = near_first(X)[:0:-1]

    peers = [(d, e) for d in z_far for e in range(X) if d or e]
    me = z * X + x

    def zat(d):
        return lax.rem(z + d, Z)

    def xat(d):
        return lax.rem(x + d, X)

    barrier = pltpu.get_barrier_semaphore()

    def greet(device):
        pl.semaphore_signal(
            barrier, inc=1, device_id=device, device_id_type=pl.DeviceIdType.MESH
        )

    for d in z_far:
        greet((nxt, zat(d), x))
        greet((prv, zat(d), x))
    for d, e in peers:
        greet((s, zat(d), xat(e)))

    load_w = pltpu.make_async_copy(w_hbm, w, w_sem)
    load_w.start()
    z_slot = [zat(d) for d in near]
    u_rows = jnp.broadcast_to(u[...], (16, LANES)).astype(jnp.bfloat16)

    def left_block(zi, carry):
        for xi in range(X):
            turned = w[zi * X + xi].T
            w_turned[zi * X + xi] = turned
            block = jnp.dot(u_rows, turned, preferred_element_type=jnp.float32)
            left_x[xi, zi] = block[0:1]
        return carry

    load_w.wait()
    lax.fori_loop(0, Z, left_block, 0)
    pl.semaphore_wait(barrier, 2 * Z + len(peers))

    def send_features(m, carry):
        for d in z_far:
            k = slot_of[(Z - d) % Z]
            remote(
                feat.at[m], hid.at[m, x, k], fz_send.at[m], fz_recv.at[m, group_of[k]],
                (nxt, zat(d), x),
            ).start()
        return carry

    early = min(2, n)

    @pl.when(s == S - 1)
    def _():
        lax.fori_loop(0, early, send_features, 0)

    def spread_z(src, dst, k):
        for d in z_far:
            if d:
                remote(src(d), dst, small_send.at[k], small_recv.at[k], (s, zat(d), x)).start()

    def share(row, send, recv):
        for d, e in peers:
            remote(row, row, send, recv, (s, zat(d), xat(e))).start()

    def spread_x(src, dst, k):
        for d in range(1, X):
            remote(src(d), dst, small_send.at[k], small_recv.at[k], (s, z, xat(d))).start()

    spread_x(lambda d: left_x.at[xat(d)], left_xin.at[x], 0)
    await_bytes(left_xin.at[pl.ds(0, X - 1)], small_recv.at[0])
    column = left_x[x]
    for d in range(1, X):
        column = column + left_xin[xat(d)]
    left_zin[z] = column
    spread_z(lambda d: left_zin.at[z], left_zin.at[z], 1)

    def forward_columns(m):
        for g, (first, size) in enumerate(groups):
            slots = pl.ds(first, size)
            await_bytes(hid.at[m, x, slots], fz_recv.at[m, g])
            for d in x_far:
                remote(
                    hid.at[m, x, slots], hid.at[m, x, slots], fx_send.at[m], fx_recv.at[m, g],
                    (s, z, xat(d)),
                ).start()

    await_bytes(left_zin.at[pl.ds(0, Z - 1)], small_recv.at[1])
    left_all[x] = jnp.sum(left_zin[...], axis=0)
    spread_x(lambda d: left_all.at[x], left_all.at[x], 3)

    @pl.when(s == S - 1)
    def _():
        lax.fori_loop(early, n, send_features, 0)

    await_bytes(left_all.at[pl.ds(0, X - 1)], small_recv.at[3])

    left = left_all[...]
    total = jnp.sum(jnp.sum(left * left, axis=(0, 1)), axis=-1, keepdims=True)
    scale_v = lax.rsqrt(total + tiny_eps)

    def pair(ref_rows):
        return jnp.concatenate(ref_rows, axis=1)

    def w_pair(xi, zi):
        return jnp.concatenate([w[zi * X + xi], w[(zi + 1) * X + xi]], axis=0)

    def right_block(zp, acc):
        zi = zp * 2
        for xi in range(X):
            rows = [
                jnp.broadcast_to(left_all[xi, zi + k] * scale_v, (16, LANES)).astype(jnp.bfloat16)
                for k in range(2)
            ]
            acc = acc + jnp.dot(pair(rows), w_pair(xi, zi), preferred_element_type=jnp.float32)
        return acc

    right = lax.fori_loop(0, Z // 2, right_block, jnp.zeros((16, LANES), jnp.float32))[0:1]

    norms[me] = right * right
    share(norms.at[me], small_send.at[4], small_recv.at[4])

    @pl.when(s == 0)
    def _():
        def pass_on(m, carry):
            forward_columns(m)
            return carry

        lax.fori_loop(0, early, pass_on, 0)

    await_bytes(norms.at[pl.ds(0, Z * X - 1)], small_recv.at[4])
    norm_total = jnp.sum(jnp.sum(norms[...], axis=0), axis=-1, keepdims=True)
    inv = 1.0 / jnp.sqrt(norm_total + tiny_eps)
    inv_sig[...] = jnp.broadcast_to(inv, (1, LANES))
    nu_out[...] = right * inv

    def forward_end(m):
        def partial_dots(acc, d, first, size):
            xi = xat(d)
            for k in range(first, first + size, 2):
                rows = jnp.concatenate([hid[m, xi, k], hid[m, xi, k + 1]], axis=1)
                cols = jnp.concatenate(
                    [w[z_slot[k] * X + xi], w[z_slot[k + 1] * X + xi]], axis=0
                )
                acc = acc + jnp.dot(rows, cols, preferred_element_type=jnp.float32)
            return acc

        acc = partial_dots(jnp.zeros((R, LANES), jnp.float32), 0, 0, Z)
        for g, (first, size) in enumerate(groups):
            await_bytes(hid.at[m, pl.ds(0, X - 1), pl.ds(first, size)], fx_recv.at[m, g])
            for d in range(1, X):
                acc = partial_dots(acc, d, first, size)
        pre_act = acc * inv_sig[...]
        pre[m] = pre_act
        out = (hid[m, x, 0].astype(jnp.float32) + pre_act * jax.nn.sigmoid(pre_act)).astype(
            jnp.bfloat16
        )
        hout[m] = out

        @pl.when(s < S - 1)
        def _():
            for d in z_far:
                k = slot_of[(Z - d) % Z]
                remote(
                    hout.at[m], hid.at[m, x, k], fz_send.at[m], fz_recv.at[m, group_of[k]],
                    (nxt, zat(d), x),
                ).start()

        @pl.when(s == S - 1)
        def _():
            terms = jnp.sum(out.astype(jnp.float32) * head[...], axis=1, keepdims=True)
            lane = lax.broadcasted_iota(jnp.int32, (R, LANES), 1)
            row = lax.broadcasted_iota(jnp.int32, (R, LANES), 0)
            spread = jnp.where(lane == row, jnp.broadcast_to(terms, (R, LANES)), 0.0)
            logits[m, me] = jnp.sum(spread, axis=0, keepdims=True)
            share(logits.at[m, me], lz_send.at[m], lz_recv.at[m])

    def backward_start(m):
        @pl.when(s == S - 1)
        def _():
            await_bytes(logits.at[m, pl.ds(0, Z * X - 1)], lz_recv.at[m])
            logit_row = jnp.sum(logits[m], axis=0)

            def as_column(row_vals, offset):
                width = row_vals.shape[1]
                lane = lax.broadcasted_iota(jnp.int32, (R, width), 1)
                row = lax.broadcasted_iota(jnp.int32, (R, width), 0)
                spread = jnp.broadcast_to(row_vals, (R, width))
                return jnp.sum(
                    jnp.where(lane == row + offset, spread, 0.0), axis=1, keepdims=True
                )

            cuts = labels.shape[1] // R
            label_row = labels[pl.ds(m // cuts, 1), :].astype(jnp.float32)
            sign = 2.0 * as_column(label_row, lax.rem(m, cuts) * R) - 1.0
            logit = as_column(logit_row, 0)
            top = -loss_scale * sign * jax.nn.sigmoid(-sign * logit)
            ghid[m] = (top * head[...]).astype(jnp.bfloat16)

        @pl.when(s < S - 1)
        def _():
            await_bytes(col_in.at[m], bz_recv.at[m])
            await_bytes(gh_in.at[m], bg_recv.at[m])
            back = jnp.sum(col_in[m].astype(jnp.float32), axis=0)
            ghid[m] = (gh_in[m].astype(jnp.float32) + back).astype(jnp.bfloat16)

        grad = (ghid[m].astype(jnp.float32) * silu_slope(pre[m])).astype(jnp.bfloat16)
        gpre[m] = grad

        @pl.when(s > 0)
        def _():
            remote(
                ghid.at[m], gh_in.at[m], bg_send.at[m], bg_recv.at[m], (prv, z, x)
            ).start()
            for g, (first, size) in reversed(list(enumerate(groups))):
                slots = pl.ds(first, size)
                for d in [*x_far, 0]:
                    xi = xat(d)
                    for k in range(first, first + size):
                        part[m, xi, k] = jnp.dot(
                            grad, w_turned[z_slot[k] * X + xi],
                            preferred_element_type=jnp.float32,
                        ).astype(jnp.bfloat16)
                    if d:
                        remote(
                            part.at[m, xi, slots], part_in.at[m, x, slots], bx_send.at[m],
                            bx_recv.at[m, g], (s, z, xi),
                        ).start()

    def backward_end(m):
        @pl.when(s > 0)
        def _():
            for g, (first, size) in reversed(list(enumerate(groups))):
                await_bytes(
                    part_in.at[m, pl.ds(0, X - 1), pl.ds(first, size)], bx_recv.at[m, g]
                )
                order = range(first + size - 1, first - 1, -1)
                for k in order:
                    column_sum = part[m, x, k].astype(jnp.float32)
                    for e in range(1, X):
                        column_sum = column_sum + part_in[m, xat(e), k].astype(jnp.float32)
                    colsum[m, k] = (column_sum * inv_sig[...]).astype(jnp.bfloat16)
                for k in order:
                    remote(
                        colsum.at[m, k], col_in.at[m, z], bz_send.at[m], bz_recv.at[m],
                        (prv, z_slot[k], x),
                    ).start()

    turns_apart = jnp.where(s == S - 1, min(3, n), n)

    def turn(t, carry):
        back = t - turns_apart

        @pl.when(t + ahead < n)
        def _():
            forward_columns(t + ahead)

        @pl.when((back >= 0) & (back < n))
        def _():
            backward_start(back)

        @pl.when(t < n)
        def _():
            forward_end(t)

        @pl.when((back >= 1) & (back <= n))
        def _():
            backward_end(back - 1)

        return carry

    ahead = jnp.where(s == 0, early, 1)

    @pl.when(s > 0)
    def _():
        forward_columns(0)

    lax.fori_loop(0, 2 * n + 1, turn, 0)

    inner = jnp.sum(gpre[...].astype(jnp.float32) * pre[...], axis=0)
    coefs[me] = jnp.sum(inner, axis=0, keepdims=True)
    share(coefs.at[me], small_send.at[6], small_recv.at[6])

    grads = gpre[...].reshape(n * R, LANES)

    def weight_block(k, zi):
        for xi in range(X):
            rows = hid[:, xi, k].reshape(n * R, LANES)
            block = lax.dot_general(
                rows, grads, (((0,), (0,)), ((), ())), preferred_element_type=jnp.float32
            )
            wg_out[zi * X + xi] = (block * inv_sig[...]).astype(jnp.bfloat16)

    for k in range(Z):
        weight_block(k, z_slot[k])

    await_bytes(coefs.at[pl.ds(0, Z * X - 1)], small_recv.at[6])
    inner_total = jnp.sum(jnp.sum(coefs[...], axis=0), axis=-1, keepdims=True)
    coef_out[...] = inner_total * inv_sig[...]

    await_bytes(left_xin.at[pl.ds(0, X - 1)], small_send.at[0])
    await_bytes(left_zin.at[pl.ds(0, Z - 1)], small_send.at[1])
    await_bytes(left_xin.at[pl.ds(0, X - 1)], small_send.at[3])
    await_bytes(norms.at[pl.ds(0, Z * X - 1)], small_send.at[4])
    await_bytes(coefs.at[pl.ds(0, Z * X - 1)], small_send.at[6])

    def drain(m, carry):
        await_bytes(hid.at[m, 0], fz_send.at[m])
        await_bytes(hid.at[m, pl.ds(0, X - 1)], fx_send.at[m])

        @pl.when(s > 0)
        def _():
            await_bytes(ghid.at[m], bg_send.at[m])
            await_bytes(part_in.at[m, pl.ds(0, X - 1)], bx_send.at[m])
            await_bytes(colsum.at[m], bz_send.at[m])

        @pl.when(s == S - 1)
        def _():
            await_bytes(logits.at[m, pl.ds(0, Z * X - 1)], lz_send.at[m])

        return carry

    lax.fori_loop(0, n, drain, 0)


def on_device(features, labels, weights, vectors, head_weight):
    S, Z, X = lax.axis_size("section"), lax.axis_size("mp_0"), lax.axis_size("mp_1")
    n, R, _ = features.shape
    features = features.reshape(n * 2, R // 2, LANES)
    n, R = n * 2, R // 2
    blocks = Z * X
    bf, f32 = jnp.bfloat16, jnp.float32
    vmem = pl.BlockSpec(memory_space=pltpu.VMEM)
    dma = pltpu.SemaphoreType.DMA
    wg, nu, coef = pl.pallas_call(
        functools.partial(step_kernel, (S, Z, X, n, R)),
        out_shape=(
            pltpu.VMEM((blocks, LANES, LANES), bf),
            pltpu.VMEM((1, LANES), f32),
            pltpu.VMEM((1, LANES), f32),
        ),
        in_specs=[vmem, vmem, pl.BlockSpec(memory_space=pl.ANY), vmem, vmem],
        out_specs=(vmem, vmem, vmem),
        scratch_shapes=[
            pltpu.VMEM((blocks, LANES, LANES), bf),
            pltpu.VMEM((blocks, LANES, LANES), bf),
            dma,
            pltpu.VMEM((n, X, Z, R, LANES), bf),
            pltpu.VMEM((n, R, LANES), bf),
            pltpu.VMEM((n, R, LANES), f32),
            pltpu.VMEM((n, R, LANES), bf),
            pltpu.VMEM((n, R, LANES), bf),
            pltpu.VMEM((n, X, Z, R, LANES), bf),
            pltpu.VMEM((n, X, Z, R, LANES), bf),
            pltpu.VMEM((n, Z, R, LANES), bf),
            pltpu.VMEM((n, Z, R, LANES), bf),
            pltpu.VMEM((n, R, LANES), bf),
            pltpu.VMEM((X, Z, 1, LANES), f32),
            pltpu.VMEM((X, Z, 1, LANES), f32),
            pltpu.VMEM((Z, Z, 1, LANES), f32),
            pltpu.VMEM((X, Z, 1, LANES), f32),
            pltpu.VMEM((blocks, 1, LANES), f32),
            pltpu.VMEM((n, blocks, 1, LANES), f32),
            pltpu.VMEM((blocks, 1, LANES), f32),
            pltpu.VMEM((1, LANES), f32),
            dma((8,)),
            dma((8,)),
            dma((n,)),
            dma((n, 3)),
            dma((n,)),
            dma((n, 3)),
            dma((n,)),
            dma((n, 3)),
            dma((n,)),
            dma((n,)),
            dma((n,)),
            dma((n,)),
            dma((n,)),
            dma((n,)),
        ],
        compiler_params=pltpu.CompilerParams(collective_id=0, has_side_effects=True),
    )(
        features,
        labels,
        weights.reshape(blocks, LANES, LANES),
        vectors,
        head_weight[None],
    )
    return wg.reshape(1, blocks * LANES, LANES), nu, coef[0, :1]


def solution(mesh):
    columns = [4 if mesh.shape["mp"] == 64 else 2]
    x_size = columns[0]
    sections = mesh.shape["section"]
    torus = Mesh(
        mesh.devices.reshape(sections, mesh.shape["mp"] // x_size, x_size),
        ("section", "mp_0", "mp_1"),
    )
    placed = (P(None, None, MP), P(), P("section", None, MP), P("section", MP), P(MP))
    return jax.shard_map(
        on_device,
        mesh=torus,
        in_specs=placed,
        out_specs=(P("section", None, MP), P("section", MP), P("section")),
        check_vma=False,
    )
```
